512 devices in a mesh: section: 8 (over y), dp: 64 (over z, x, core).
Axes of the slice: x: 4, y: 8, z: 8, core: 2. Of those that a mesh axis runs over, the one named last changes fastest.
Arguments:
- fresh_acts: bfloat16 [3, 128, 8192], P(None, None, 'dp'), may hold values from -36 to 36
- carried: bfloat16 [8, 128, 8192], P('section', None, 'dp'), may hold values from -36 to 36
- norm_gain: float32 [8, 8192], P('section'), may hold values from 0.1 to 1.9
- w_in: bfloat16 [8, 3, 4096, 8192], P('section', None, 'dp'), may hold values from -0.0625 to 0.0625
- short_filter: float32 [8, 3, 4096, 3], P('section', None, 'dp'), may hold values from -3 to 3
- filter_taps: float32 [8, 4096, 128], P('section', 'dp'), may hold values from -0.9 to 0.9
- decay_rate: float32 [8, 4096], P('section', 'dp'), may hold values from 0.01 to 0.12
- w_out: bfloat16 [8, 4096, 8192], P('section', None, 'dp'), may hold values from -0.09375 to 0.09375
Outputs:
- section_outputs: bfloat16 [8, 3, 128, 8192], P('section', None, None, 'dp')
The draws below stay inside these ranges and needn't reach their ends.
All inputs are finite; a program needn't handle non-finite values.
Results may differ from the reference program's by a relative error of at most 0.011.
Values may be sent and summed in bfloat16 or wider, within the bound.
A program may use at most 64 MiB of HBM per device.

```python
import math
import jax
import jax.numpy as jnp
from jax import lax

D = 8192
CH = 4096
SHORT = 3
FLEN = 128
SEQ = 128
TICKS = 3
N_SECTION = 8


def scaled_acts(key, shape, base_vals):
    key_row = jax.random.fold_in(key, 11)
    key_col = jax.random.fold_in(key, 12)
    row_scale = jnp.exp(jax.random.uniform(key_row, shape[:-1] + (1,), jnp.float32, math.log(0.3), math.log(3.0)))
    col_scale = jnp.exp(jax.random.uniform(key_col, (shape[-1],), jnp.float32, math.log(0.3), math.log(3.0)))
    return base_vals * row_scale * col_scale


def draw_fresh_acts(key, part):
    shape = (TICKS, SEQ, D)
    key_val = jax.random.fold_in(key, 10)
    base_vals = jnp.clip(jax.random.normal(key_val, shape, jnp.float32), -4.0, 4.0)
    return scaled_acts(key, shape, base_vals).astype(jnp.bfloat16)


def draw_carried(key, part):
    shape = (N_SECTION, SEQ, D)
    key_val = jax.random.fold_in(key, 20)
    base_vals = jnp.clip(jax.random.normal(key_val, shape, jnp.float32), -4.0, 4.0)
    return scaled_acts(key, shape, base_vals).astype(jnp.bfloat16)


def block_levels(rng, dims, cuts, smallest, largest):
    loudness = 1.0
    for position, shards_of in cuts:
        heights = jax.random.uniform(jax.random.fold_in(jax.random.fold_in(rng, 6), position), (shards_of,), jnp.float32, smallest / len(cuts), largest / len(cuts))
        loudness = loudness * jnp.repeat(jnp.exp(heights), dims[position] // shards_of).reshape((-1,) + (1,) * (len(dims) - 1 - position))
    return loudness


def noise(own_key, shape, width, most, cuts=(), held_as=jnp.bfloat16):
    values = jax.random.normal(own_key, shape, jnp.float32) * width
    if len(cuts) > 0:
        values = block_levels(own_key, shape, cuts, -0.22, 0.18) * values
    return jnp.clip(values, min=-most, max=most).astype(held_as)


def setup_inputs(seed: int = 0) -> dict:
    splits = jax.random.split(jax.random.key(seed), 9)
    return {
        "fresh_acts": draw_fresh_acts(jax.random.fold_in(splits[8], 71), 0),
        "carried": draw_carried(jax.random.fold_in(splits[8], 71), 0),
        "norm_gain": jnp.clip(1.0 + 0.18 * jax.random.normal(splits[2], (N_SECTION, D), jnp.float32), 0.1, 1.9),
        "w_in": noise(splits[3], (N_SECTION, 3, CH, D), D ** -0.5, 0.0625, ((0, 8), (2, 64))),
        "short_filter": noise(splits[4], (N_SECTION, 3, CH, SHORT), 0.6, 3.0, ((0, 8), (2, 64)), jnp.float32),
        "filter_taps": noise(splits[5], (N_SECTION, CH, FLEN), 0.15, 0.9, ((0, 8), (1, 64)), jnp.float32),
        "decay_rate": jnp.clip(jnp.exp(math.log(0.12) - 2.4849066 * jax.random.uniform(splits[6], (N_SECTION, CH), jnp.float32) ** block_levels(splits[6], (N_SECTION, CH), ((0, 8), (1, 64)), -0.2, 0.2)), 0.01, 0.12),
        "w_out": noise(splits[7], (N_SECTION, CH, D), CH ** -0.5, 0.09375, ((0, 8), (2, 64))),
    }


EPS = 1e-06

def hyena_layer(acts, norm_gain, w_in, short_filter, filter_taps, decay_rate, w_out):
    widened = acts.astype(jnp.float32)
    factor = lax.rsqrt(lax.optimization_barrier(jnp.mean(widened * widened, axis=1)) + EPS)
    normed = (widened * norm_gain).astype(jnp.bfloat16)
    proj_acc = lax.dot_general(normed, w_in.reshape(3 * CH, D), (((1,), (1,)), ((), ())), preferred_element_type=jnp.float32)
    u_proj = (proj_acc * factor[:, None]).reshape(SEQ, 3, CH)
    padded = jnp.pad(u_proj, ((SHORT - 1, 0), (0, 0), (0, 0)))
    mixed_out = short_filter[:, :, 0] * u_proj
    for j in range(1, SHORT):
        mixed_out = mixed_out + short_filter[:, :, j] * padded[SHORT - 1 - j:SHORT - 1 - j + SEQ]
    query_part = mixed_out[:, 0]
    key_part = mixed_out[:, 1]
    value_part = mixed_out[:, 2]
    filter_vals = filter_taps * jnp.exp(-decay_rate[:, None] * jnp.arange(FLEN, dtype=jnp.float32)[None, :])
    product = key_part * value_part
    padded_prod = jnp.pad(product, ((FLEN - 1, 0), (0, 0)))
    long_conv = filter_vals[:, 0] * product
    for j in range(1, FLEN):
        long_conv = long_conv + filter_vals[:, j] * padded_prod[FLEN - 1 - j:FLEN - 1 - j + SEQ]
    y_local = (query_part * long_conv).astype(jnp.bfloat16)
    return (widened + jnp.dot(y_local, w_out, preferred_element_type=jnp.float32)).astype(jnp.bfloat16)

def reference(fresh_acts, carried, norm_gain, w_in, short_filter, filter_taps, decay_rate, w_out):
    results = []
    for s in range(N_SECTION):
        section_rows = []
        for k in range(TICKS):
            if s == 0:
                layer_in = fresh_acts[k]
            elif k == 0:
                layer_in = carried[s]
            else:
                layer_in = results[s - 1][k - 1]
            section_rows.append(hyena_layer(layer_in, norm_gain[s], w_in[s], short_filter[s], filter_taps[s], decay_rate[s], w_out[s]))
        results.append(section_rows)
    return jnp.stack([jnp.stack(section_rows) for section_rows in results])
```

```python
import jax
import jax.numpy as jnp
from jax import lax
from jax.experimental import pallas as pl
from jax.experimental.pallas import tpu as pltpu
from jax.sharding import PartitionSpec as P

EPS = 1e-06
MESH = pl.DeviceIdType.MESH
F32 = jnp.float32
BF16 = jnp.bfloat16

NZ, NX, NS = 8, 4, 8
NP = NZ * NX
TICKS, SEQ, FD, CD, D = 3, 128, 128, 64, 8192
Z_ORDER = (1, 7, 2, 6, 3, 5, 4)
X_ORDER = (1, 3, 2)
GROUP = 2


def kernel(
    fresh, carried, gain, w_in, taps_hbm, long_hbm, decay_hbm, w_out, out,
    acts, gated, produced, result, w1, w2raw, w2, gain_v, fresh_v, carried_v,
    taps_v, long_v, decay_v, taps_sq, taps_row, long_row, normed, acc, acc_in, u_pad, p_pad, fin_out, fin_in,
    sem_in, sem_w, sem_wsend, sem_wrecv, a_send, a_recv, y_send, y_recv, x_send, x_recv, sem_out,
):
    s = lax.axis_index("section")
    d = lax.axis_index("dp")
    z, x, c = d // 8, (d // 2) % 4, d % 2
    nxt, prv = (s + 1) % NS, (s + NS - 1) % NS

    def dev(sec, dz, dx, core):
        return (sec, ((z + dz) % NZ) * 8 + ((x + dx) % NX) * 2 + core)

    sibling = dev(s, 0, 0, 1 - c)

    def remote(src, dst, send, recv, target):
        return pltpu.make_async_remote_copy(
            src_ref=src, dst_ref=dst, send_sem=send, recv_sem=recv,
            device_id=target, device_id_type=MESH,
        )

    def piece_of(j):
        dz, dx = j // NX, j % NX
        return ((z + NZ - dz) % NZ) * NX + (x + NX - dx) % NX

    in_fresh = pltpu.make_async_copy(fresh, fresh_v, sem_in.at[0])
    in_carried = pltpu.make_async_copy(carried.at[0], carried_v, sem_in.at[1])
    in_gain = pltpu.make_async_copy(gain, gain_v, sem_in.at[2])
    in_taps = pltpu.make_async_copy(taps_hbm.at[0], taps_v, sem_in.at[3])
    in_long = pltpu.make_async_copy(long_hbm.at[0], long_v, sem_in.at[4])
    in_decay = pltpu.make_async_copy(decay_hbm, decay_v, sem_in.at[5])
    in_fresh.start()
    in_carried.start()

    barrier = pltpu.get_barrier_semaphore()
    peers = [dev(s, dz, 0, c) for dz in range(1, NZ)]
    peers += [dev(s, 0, dx, c) for dx in range(1, NX)]
    peers += [sibling]
    peers += [dev(nxt, dz, 0, c) for dz in range(NZ)]
    peers += [dev(prv, dz, 0, c) for dz in range(NZ)]
    for peer in peers:
        pl.semaphore_signal(barrier, inc=1, device_id=peer, device_id_type=MESH)
    in_gain.start()
    in_taps.start()
    in_long.start()
    in_decay.start()

    in_fresh.wait()
    in_carried.wait()
    first = s == 0
    acts[0, 0] = jnp.where(first, fresh_v[0], carried_v[...])
    pl.semaphore_wait(barrier, len(peers))

    def phase_one(buf, src, send, recv, sec, own):
        for dz in ((0,) if own else ()) + Z_ORDER:
            remote(src, buf.at[dz * NX], send, recv.at[dz * NX], dev(sec, dz, 0, c)).start()

    def arrived(buf, recv, j):
        remote(buf.at[j], buf.at[j], recv.at[j], recv.at[j], sibling).wait_recv()

    def phase_two(buf, send, recv, own):
        for dz in (0,) + Z_ORDER:
            j = dz * NX
            if dz or own:
                arrived(buf, recv, j)
            for dx in X_ORDER:
                remote(buf.at[j], buf.at[j + dx], send, recv.at[j + dx], dev(s, 0, dx, c)).start()

    def drain(buf, send, count):
        pltpu.make_async_copy(buf.at[pl.ds(0, count)], buf.at[pl.ds(0, count)], send).wait()

    phase_one(acts.at[0], acts.at[0, 0], a_send.at[0], a_recv.at[0], s, False)

    @pl.loop(0, NP)
    def _(j):
        col = pl.multiple_of(piece_of(j) * 256 + c * 128, 128)
        other = pl.multiple_of(piece_of(j) * 256 + (1 - c) * 128, 128)
        to = pl.multiple_of(j * 128, 128)
        pltpu.make_async_copy(
            w_in.at[0, :, :, pl.ds(col, 128)], w1.at[0, :, :, pl.ds(to, 128)], sem_w.at[0]
        ).start()
        remote(
            w_in.at[0, :, :, pl.ds(other, 128)], w1.at[1, :, :, pl.ds(to, 128)],
            sem_wsend.at[0], sem_wrecv.at[0], sibling,
        ).start()

    own_out = pltpu.make_async_copy(w_out.at[:, c], w2raw.at[0], sem_w.at[1])
    other_out = remote(w_out.at[:, 1 - c], w2raw.at[1], sem_wsend.at[1], sem_wrecv.at[1], sibling)
    own_out.start()
    other_out.start()

    phase_two(acts.at[0], a_send.at[0], a_recv.at[0], False)

    lane = lax.broadcasted_iota(jnp.int32, (64, 128), 1)
    in_taps.wait()
    in_long.wait()
    in_decay.wait()
    in_gain.wait()
    taps_sq[...] = jnp.zeros_like(taps_sq)
    for i in range(3):
        taps_sq[pl.ds(i * 64, 64), pl.ds(0, 3)] = taps_v[i]
    for half in range(2):
        turned = taps_sq[pl.ds(half * 128, 128), :].T
        taps_row[:, pl.ds(half * 128, 128)] = turned[0:8]
    long_tall = jnp.concatenate([long_v[...], long_v[...]], axis=0).T
    decay_v2 = jnp.concatenate([decay_v[...], decay_v[...]], axis=1)
    lag = lax.broadcasted_iota(jnp.int32, (64, 128), 0) + jnp.where(lane < 64, 0, 64)
    long_row[...] = jnp.where(lane < 64, long_tall[0:64], long_tall[64:128]) * jnp.exp(
        -decay_v2 * lag.astype(F32)
    )
    u_pad[pl.ds(0, 8), :] = jnp.zeros((8, 256), F32)
    p_pad[pl.ds(0, 64), :] = jnp.zeros((64, 128), F32)

    own_out.wait()
    other_out.wait_recv()
    for o in range(2):
        for jp in range(NP // 2):
            two = jnp.concatenate(
                [w2raw[o, piece_of(2 * jp)], w2raw[o, piece_of(2 * jp + 1)]], axis=0
            )
            w2[pl.ds(o * 128, 128), pl.ds(jp * 128, 128)] = two.astype(F32).T.astype(BF16)

    pltpu.make_async_copy(w1.at[0], w1.at[0], sem_w.at[0]).wait()
    remote(w1.at[1], w1.at[1], sem_wsend.at[0], sem_wrecv.at[0], sibling).wait_recv()

    lane128 = lax.broadcasted_iota(jnp.int32, (128, 128), 1)
    low = lane128 < 64

    for k in range(TICKS):
        buf, recv = acts.at[k], a_recv.at[k]
        if k:
            phase_two(buf, a_send.at[k], recv, True)
        squares = jnp.zeros((SEQ, FD), F32)
        slabs = (0,) + Z_ORDER
        for g in range(NZ // GROUP):
            keys = []
            for dz in slabs[g * GROUP:(g + 1) * GROUP]:
                for dx in (0,) + X_ORDER:
                    j = dz * NX + dx
                    if dx:
                        arrived(buf, recv, j)
                    wide = buf[j].astype(F32)
                    col = pl.multiple_of(piece_of(j) * 256 + c * 128, 128)
                    normed[:, pl.ds(j * 128, 128)] = (wide * gain_v[:, pl.ds(col, 128)]).astype(BF16)
                    squares = squares + wide * wide
                keys.append(dz)
            for o in range(2):
                part = None
                for dz in keys:
                    cols = pl.ds(dz * NX * 128, NX * 128)
                    w = w1[o, :, :, cols].reshape(3 * CD, NX * 128)
                    term = lax.dot_general(
                        normed[:, cols], w, (((1,), (1,)), ((), ())), preferred_element_type=F32
                    )
                    part = term if part is None else part + term
                cols192 = pl.ds(0, 192)
                if g == 0:
                    acc[o, :, cols192] = part
                else:
                    acc[o, :, cols192] = acc[o, :, cols192] + part
        row_sq = jnp.sum(squares, axis=1, keepdims=True)
        acc[1, :, pl.ds(192, 64)] = jnp.broadcast_to(row_sq, (SEQ, 64))
        swap = remote(acc.at[1], acc_in.at[k], x_send.at[2 * k], x_recv.at[2 * k], sibling)
        swap.start()
        swap.wait_recv()
        total_sq = row_sq + acc_in[k, :, pl.ds(192, 1)]
        factor = lax.rsqrt(total_sq / D + EPS)
        u_pad[pl.ds(8, SEQ), :] = (acc[0] + acc_in[k]) * factor
        mixed = taps_row[0:1, :] * u_pad[pl.ds(8, SEQ), :]
        for j in range(1, 3):
            mixed = mixed + taps_row[j:j + 1, :] * u_pad[pl.ds(8 - j, SEQ), :]
        left, right = mixed[:, 0:128], mixed[:, 128:256]
        p_low = pltpu.roll(left, 64, 1) * right
        p_high = left * pltpu.roll(right, 64, 1)
        p_pad[pl.ds(64, 64), :] = jnp.where(low[0:64], p_low[0:64], 0.0)
        p_pad[pl.ds(128, 64), :] = jnp.where(low[0:64], p_low[64:128], p_high[0:64])
        conv = jnp.zeros((SEQ, 128), F32)
        for j in range(64):
            conv = conv + long_row[j:j + 1, :] * p_pad[pl.ds(64 - j, SEQ), :]
        y = left * (conv + pltpu.roll(conv, 64, 1))
        gbuf, grecv = gated.at[k], y_recv.at[k]
        gated[k, 0] = y.T[0:64].astype(BF16)
        swap.wait_send()

        phase_one(gbuf, gbuf.at[0], y_send.at[k], grecv, s, False)
        phase_two(gbuf, y_send.at[k], grecv, False)
        total = None
        for g in range(NZ // GROUP):
            for dz in slabs[g * GROUP:(g + 1) * GROUP]:
                for dx in X_ORDER:
                    arrived(gbuf, grecv, dz * NX + dx)
            for dz in slabs[g * GROUP:(g + 1) * GROUP]:
                rhs = gated[k, pl.ds(dz * NX, NX)].reshape(NX * CD, SEQ)
                term = jnp.dot(
                    w2[:, pl.ds(dz * NX * CD, NX * CD)], rhs, preferred_element_type=F32
                )
                total = term if total is None else total + term
        fin_out[...] = total[128:256]
        swap2 = remote(fin_out, fin_in.at[k], x_send.at[2 * k + 1], x_recv.at[2 * k + 1], sibling)
        swap2.start()
        swap2.wait_recv()
        final = (total[0:128] + fin_in[k]).T + acts[k, 0].astype(F32)
        final = final.astype(BF16)
        result[k] = final
        if k + 1 < TICKS:
            produced[k] = jnp.where(s == NS - 1, fresh_v[k + 1], final)
            phase_one(
                acts.at[k + 1], produced.at[k], a_send.at[k + 1], a_recv.at[k + 1], nxt, True
            )
        swap2.wait_send()

    put = pltpu.make_async_copy(result, out.at[0], sem_out)
    put.start()
    pltpu.make_async_copy(w1.at[0], w1.at[0], sem_wsend.at[0]).wait()
    other_out.wait_send()
    for k in range(TICKS):
        drain(acts.at[k], a_send.at[k], NP if k else NP - 1)
        drain(gated.at[k], y_send.at[k], NP - 1)
    put.wait()


def body(fresh_acts, carried, norm_gain, w_in, short_filter, filter_taps, decay_rate, w_out):
    w_out4 = w_out.reshape(NP, 2, CD, FD)
    any_spec = pl.BlockSpec(memory_space=pl.ANY)
    dma = pltpu.SemaphoreType.DMA
    return pl.pallas_call(
        kernel,
        name="relay",
        out_shape=jax.ShapeDtypeStruct((1, TICKS, SEQ, FD), BF16),
        in_specs=[any_spec] * 8,
        out_specs=any_spec,
        scratch_shapes=[
            pltpu.VMEM((TICKS, NP, SEQ, FD), BF16),
            pltpu.VMEM((TICKS, NP, CD, SEQ), BF16),
            pltpu.VMEM((TICKS - 1, SEQ, FD), BF16),
            pltpu.VMEM((TICKS, SEQ, FD), BF16),
            pltpu.VMEM((2, 3, CD, NP * 128), BF16),
            pltpu.VMEM((2, NP, CD, FD), BF16),
            pltpu.VMEM((256, NP * CD), BF16),
            pltpu.VMEM((1, D), F32),
            pltpu.VMEM((TICKS, SEQ, FD), BF16),
            pltpu.VMEM((SEQ, FD), BF16),
            pltpu.VMEM((3, CD, 3), F32),
            pltpu.VMEM((CD, 128), F32),
            pltpu.VMEM((1, CD), F32),
            pltpu.VMEM((256, 128), F32),
            pltpu.VMEM((8, 256), F32),
            pltpu.VMEM((64, 128), F32),
            pltpu.VMEM((SEQ, NP * 128), BF16),
            pltpu.VMEM((2, SEQ, 256), F32),
            pltpu.VMEM((TICKS, SEQ, 256), F32),
            pltpu.VMEM((8 + SEQ, 256), F32),
            pltpu.VMEM((64 + SEQ, 128), F32),
            pltpu.VMEM((FD, SEQ), F32),
            pltpu.VMEM((TICKS, FD, SEQ), F32),
            dma((6,)),
            dma((2,)),
            dma((2,)),
            dma((2,)),
            dma((TICKS,)),
            dma((TICKS, NP)),
            dma((TICKS,)),
            dma((TICKS, NP)),
            dma((2 * TICKS,)),
            dma((2 * TICKS,)),
            dma(()),
        ],
        compiler_params=pltpu.CompilerParams(
            collective_id=0, has_side_effects=True, vmem_limit_bytes=56 << 20
        ),
    )(fresh_acts, carried, norm_gain, w_in, short_filter, filter_taps, decay_rate, w_out4)


def solution(mesh):
    return jax.shard_map(
        body,
        mesh=mesh,
        in_specs=(
            P(None, None, "dp"),
            P("section", None, "dp"),
            P("section", None),
            P("section", None, "dp", None),
            P("section", None, "dp", None),
            P("section", "dp", None),
            P("section", "dp"),
            P("section", None, "dp"),
        ),
        out_specs=P("section", None, None, "dp"),
        check_vma=False,
    )
```

```python
import jax
import jax.numpy as jnp
from jax import lax
from jax.experimental import pallas as pl
from jax.experimental.pallas import tpu as pltpu
from jax.sharding import PartitionSpec as P

EPS = 1e-06
MESH = pl.DeviceIdType.MESH
F32 = jnp.float32
BF16 = jnp.bfloat16

NZ, NX, NS = 8, 4, 8
NP = NZ * NX
TICKS, SEQ, FD, CD, D = 3, 128, 128, 64, 8192
NH, HT = 2, 64
Z_ORDER = (1, 7, 2, 6, 3, 5, 4)
X_ORDER = (1, 3, 2)
SLABS = (0,) + Z_ORDER


def kernel(
    fresh, carried, gain, w_in, taps_hbm, long_hbm, decay_hbm, w_out, out,
    acts, gated, produced, result, w1, w2raw, w2, gain_v, fresh_v, carried_v,
    taps_v, long_v, decay_v, taps_row, long_row, normed, acc, acc_in, u_pad, p_pad, fin_out, fin_in,
    sem_in, sem_w, sem_wsend, sem_wrecv, a_send, a_recv, y_send, y_recv, u_send, u_recv, f_send, f_recv, sem_out,
):
    s = lax.axis_index("section")
    d = lax.axis_index("dp")
    z, x, c = d // 8, (d // 2) % 4, d % 2
    nxt, prv = (s + 1) % NS, (s + NS - 1) % NS

    def dev(sec, dz, dx, core):
        return (sec, ((z + dz) % NZ) * 8 + ((x + dx) % NX) * 2 + core)

    sibling = dev(s, 0, 0, 1 - c)

    def remote(src, dst, send, recv, target):
        return pltpu.make_async_remote_copy(
            src_ref=src, dst_ref=dst, send_sem=send, recv_sem=recv,
            device_id=target, device_id_type=MESH,
        )

    def piece_of(j):
        dz, dx = j // NX, j % NX
        return ((z + NZ - dz) % NZ) * NX + (x + NX - dx) % NX

    in_fresh = pltpu.make_async_copy(fresh, fresh_v, sem_in.at[0])
    in_carried = pltpu.make_async_copy(carried.at[0], carried_v, sem_in.at[1])
    in_gain = pltpu.make_async_copy(gain, gain_v, sem_in.at[2])
    in_taps = pltpu.make_async_copy(taps_hbm, taps_v, sem_in.at[3])
    in_long = pltpu.make_async_copy(long_hbm.at[0], long_v, sem_in.at[4])
    in_decay = pltpu.make_async_copy(decay_hbm, decay_v, sem_in.at[5])
    in_fresh.start()
    in_carried.start()

    barrier = pltpu.get_barrier_semaphore()
    peers = [dev(s, dz, 0, c) for dz in range(1, NZ)]
    peers += [dev(s, 0, dx, c) for dx in range(1, NX)]
    peers += [sibling]
    peers += [dev(nxt, dz, 0, c) for dz in range(NZ)]
    peers += [dev(prv, dz, 0, c) for dz in range(NZ)]
    for peer in peers:
        pl.semaphore_signal(barrier, inc=1, device_id=peer, device_id_type=MESH)
    in_gain.start()
    in_taps.start()
    in_long.start()
    in_decay.start()

    in_fresh.wait()
    in_carried.wait()
    start = jnp.where(s == 0, fresh_v[0], carried_v[...])
    for h in range(NH):
        acts[0, h, 0] = start[h * HT:(h + 1) * HT]
    pl.semaphore_wait(barrier, len(peers))

    def phase_one(buf, src, send, recv, sec, own):
        for dz in SLABS if own else Z_ORDER:
            remote(src, buf.at[dz * NX], send, recv.at[dz * NX], dev(sec, dz, 0, c)).start()

    def arrived(buf, recv, j):
        remote(buf.at[j], buf.at[j], recv.at[j], recv.at[j], sibling).wait_recv()

    def phase_two(buf, send, recv, own, slabs):
        for dz in slabs:
            j = dz * NX
            if dz or own:
                arrived(buf, recv, j)
            for dx in X_ORDER:
                remote(buf.at[j], buf.at[j + dx], send, recv.at[j + dx], dev(s, 0, dx, c)).start()

    def drain(buf, send, count):
        pltpu.make_async_copy(buf.at[pl.ds(0, count)], buf.at[pl.ds(0, count)], send).wait()

    for h in range(NH):
        phase_one(acts.at[0, h], acts.at[0, h, 0], a_send.at[0, h], a_recv.at[0, h], s, False)

    @pl.loop(0, NP)
    def _(j):
        col = pl.multiple_of(piece_of(j) * 256 + c * 128, 128)
        other = pl.multiple_of(piece_of(j) * 256 + (1 - c) * 128, 128)
        to = pl.multiple_of(j * 128, 128)
        pltpu.make_async_copy(
            w_in.at[0, :, :, pl.ds(col, 128)], w1.at[0, :, :, pl.ds(to, 128)], sem_w.at[0]
        ).start()
        remote(
            w_in.at[0, :, :, pl.ds(other, 128)], w1.at[1, :, :, pl.ds(to, 128)],
            sem_wsend.at[0], sem_wrecv.at[0], sibling,
        ).start()

    own_out = pltpu.make_async_copy(w_out.at[:, c], w2raw.at[0], sem_w.at[1])
    other_out = remote(w_out.at[:, 1 - c], w2raw.at[1], sem_wsend.at[1], sem_wrecv.at[1], sibling)
    own_out.start()
    other_out.start()

    for h in range(NH):
        phase_two(acts.at[0, h], a_send.at[0, h], a_recv.at[0, h], False, SLABS)

    lane = lax.broadcasted_iota(jnp.int32, (64, 128), 1)
    low = lane < 64
    in_taps.wait()
    in_long.wait()
    in_decay.wait()
    in_gain.wait()
    for j in range(3):
        taps_row[pl.ds(j, 1), pl.ds(0, 128)] = jnp.concatenate([taps_v[0, j], taps_v[1, j]], axis=1)
        taps_row[pl.ds(j, 1), pl.ds(128, 128)] = jnp.concatenate([taps_v[2, j], taps_v[2, j]], axis=1)
    long_tall = jnp.concatenate([long_v[...], long_v[...]], axis=0).T
    decay_v2 = jnp.concatenate([decay_v[...], decay_v[...]], axis=1)
    lag = lax.broadcasted_iota(jnp.int32, (64, 128), 0) + jnp.where(low, 0, 64)
    long_row[...] = jnp.where(low, long_tall[0:64], long_tall[64:128]) * jnp.exp(
        -decay_v2 * lag.astype(F32)
    )

    own_out.wait()
    other_out.wait_recv()
    for o in range(2):
        for jp in range(NZ):
            pieces = [w2raw[o, piece_of(NX * jp + i)].astype(F32) for i in range(NX)]
            for part in range(2):
                four = jnp.concatenate([p[part * 32:part * 32 + 32] for p in pieces], axis=0)
                w2[pl.ds(part * 256 + o * 128, 128), pl.ds(jp * 128, 128)] = four.T.astype(BF16)

    pltpu.make_async_copy(w1.at[0], w1.at[0], sem_w.at[0]).wait()
    remote(w1.at[1], w1.at[1], sem_wsend.at[0], sem_wrecv.at[0], sibling).wait_recv()

    for k in range(TICKS):
        u_pad[k, pl.ds(0, 8), :] = jnp.zeros((8, 256), F32)
        p_pad[k, pl.ds(0, 64), :] = jnp.zeros((64, 128), F32)

    swaps = {}

    def spread(k, h, slabs):
        phase_two(acts.at[k, h], a_send.at[k, h], a_recv.at[k, h], k > 0, slabs)

    def project(k, h):
        buf, recv = acts.at[k, h], a_recv.at[k, h]
        squares = jnp.zeros((HT, FD), F32)
        for n, dz in enumerate(SLABS):
            for dx in (0,) + X_ORDER:
                j = dz * NX + dx
                if dx:
                    arrived(buf, recv, j)
                wide = buf[j].astype(F32)
                col = pl.multiple_of(piece_of(j) * 256 + c * 128, 128)
                normed[h, :, pl.ds(j * 128, 128)] = (wide * gain_v[:, pl.ds(col, 128)]).astype(BF16)
                squares = squares + wide * wide
            cols = pl.ds(dz * NX * 128, NX * 128)
            lhs = normed[h, :, cols]
            for o in range(2):
                w = w1[o, :, :, cols].reshape(3 * CD, NX * 128)
                term = lax.dot_general(
                    lhs, w, (((1,), (1,)), ((), ())), preferred_element_type=F32
                )
                if n == 0:
                    acc[k, h, o, :, pl.ds(0, 192)] = term
                else:
                    acc[k, h, o, :, pl.ds(0, 192)] = acc[k, h, o, :, pl.ds(0, 192)] + term
        row_sq = jnp.sum(squares, axis=1, keepdims=True)
        for o in range(2):
            acc[k, h, o, :, pl.ds(192, 64)] = jnp.broadcast_to(row_sq, (HT, 64))
        swaps[k, h, 0] = remote(
            acc.at[k, h, 1], acc_in.at[k, h], u_send.at[k, h], u_recv.at[k, h], sibling
        )
        swaps[k, h, 0].start()

    def mix(k, h):
        swaps[k, h, 0].wait_recv()
        both = acc[k, h, 0] + acc_in[k, h]
        factor = lax.rsqrt(both[:, 192:193] / D + EPS)
        row = 8 + h * HT
        u_pad[k, pl.ds(row, HT), :] = both * factor
        mixed = taps_row[0:1, :] * u_pad[k, pl.ds(row, HT), :]
        for j in range(1, 3):
            mixed = mixed + taps_row[j:j + 1, :] * u_pad[k, pl.ds(row - j, HT), :]
        left, right = mixed[:, 0:128], mixed[:, 128:256]
        p_low = pltpu.roll(left, 64, 1) * right
        if h == 0:
            p_pad[k, pl.ds(64, 64), :] = jnp.where(low, p_low, 0.0)
            p_pad[k, pl.ds(128, 64), :] = jnp.where(low, 0.0, left * pltpu.roll(right, 64, 1))
        else:
            p_pad[k, pl.ds(128, 64), :] = jnp.where(low, p_low, p_pad[k, pl.ds(128, 64), :])
        conv = jnp.zeros((HT, 128), F32)
        for j in range(64):
            conv = conv + long_row[j:j + 1, :] * p_pad[k, pl.ds(64 + h * HT - j, HT), :]
        y = left * (conv + pltpu.roll(conv, 64, 1))
        tall = jnp.concatenate([y, pltpu.roll(y, 96, 1)], axis=0).T
        gated[k, h, 0] = tall[0:32].astype(BF16)
        phase_one(gated.at[k, h], gated.at[k, h, 0], y_send.at[k, h], y_recv.at[k, h], s, False)

    def spread_gated(k, h, slabs):
        phase_two(gated.at[k, h], y_send.at[k, h], y_recv.at[k, h], False, slabs)

    def combine(k, h):
        buf, recv = gated.at[k, h], y_recv.at[k, h]
        total = None
        for g in range(4):
            for dz in SLABS[2 * g:2 * g + 2]:
                for dx in X_ORDER:
                    arrived(buf, recv, dz * NX + dx)
            for dz in SLABS[2 * g:2 * g + 2]:
                rhs = gated[k, h, pl.ds(dz * NX, NX)].reshape(NX * 32, 128)
                term = jnp.dot(w2[:, pl.ds(dz * 128, 128)], rhs, preferred_element_type=F32)
                total = term if total is None else total + term
        folded = total[0:256] + pltpu.roll(total[256:512], 64, 1)
        fin_out[k, h, 0] = folded[0:128].T[0:HT]
        fin_out[k, h, 1] = folded[128:256].T[0:HT]
        swaps[k, h, 1] = remote(
            fin_out.at[k, h, 1], fin_in.at[k, h], f_send.at[k, h], f_recv.at[k, h], sibling
        )
        swaps[k, h, 1].start()

    def finish(k, h):
        swaps[k, h, 1].wait_recv()
        rows = pl.ds(h * HT, HT)
        final = (fin_out[k, h, 0] + fin_in[k, h]) + acts[k, h, 0].astype(F32)
        final = final.astype(BF16)
        result[k, rows] = final
        if k + 1 < TICKS:
            produced[k, h] = jnp.where(s == NS - 1, fresh_v[k + 1, rows], final)
            phase_one(
                acts.at[k + 1, h], produced.at[k, h], a_send.at[k + 1, h], a_recv.at[k + 1, h], nxt, True
            )

    for k in range(TICKS):
        if k:
            spread(k, 0, SLABS)
            spread(k, 1, SLABS)
        project(k, 0)
        mix(k, 0)
        project(k, 1)
        mix(k, 1)
        spread_gated(k, 0, SLABS)
        spread_gated(k, 1, SLABS)
        combine(k, 0)
        finish(k, 0)
        combine(k, 1)
        finish(k, 1)

    put = pltpu.make_async_copy(result, out.at[0], sem_out)
    put.start()
    pltpu.make_async_copy(w1.at[0], w1.at[0], sem_wsend.at[0]).wait()
    other_out.wait_send()
    for swap in swaps.values():
        swap.wait_send()
    for k in range(TICKS):
        for h in range(NH):
            drain(acts.at[k, h], a_send.at[k, h], NP if k else NP - 1)
            drain(gated.at[k, h], y_send.at[k, h], NP - 1)
    put.wait()


def body(fresh_acts, carried, norm_gain, w_in, short_filter, filter_taps, decay_rate, w_out):
    w_out4 = w_out.reshape(NP, 2, CD, FD)
    taps = jnp.transpose(short_filter, (1, 3, 0, 2))
    any_spec = pl.BlockSpec(memory_space=pl.ANY)
    dma = pltpu.SemaphoreType.DMA
    return pl.pallas_call(
        kernel,
        name="relay",
        out_shape=jax.ShapeDtypeStruct((1, TICKS, SEQ, FD), BF16),
        in_specs=[any_spec] * 8,
        out_specs=any_spec,
        scratch_shapes=[
            pltpu.VMEM((TICKS, NH, NP, HT, FD), BF16),
            pltpu.VMEM((TICKS, NH, NP, 32, 128), BF16),
            pltpu.VMEM((TICKS - 1, NH, HT, FD), BF16),
            pltpu.VMEM((TICKS, SEQ, FD), BF16),
            pltpu.VMEM((2, 3, CD, NP * 128), BF16),
            pltpu.VMEM((2, NP, CD, FD), BF16),
            pltpu.VMEM((512, NP * 32), BF16),
            pltpu.VMEM((1, D), F32),
            pltpu.VMEM((TICKS, SEQ, FD), BF16),
            pltpu.VMEM((SEQ, FD), BF16),
            pltpu.VMEM((3, 3, 1, CD), F32),
            pltpu.VMEM((CD, 128), F32),
            pltpu.VMEM((1, CD), F32),
            pltpu.VMEM((8, 256), F32),
            pltpu.VMEM((64, 128), F32),
            pltpu.VMEM((NH, HT, NP * 128), BF16),
            pltpu.VMEM((TICKS, NH, 2, HT, 256), F32),
            pltpu.VMEM((TICKS, NH, HT, 256), F32),
            pltpu.VMEM((TICKS, 8 + SEQ, 256), F32),
            pltpu.VMEM((TICKS, 64 + SEQ, 128), F32),
            pltpu.VMEM((TICKS, NH, 2, HT, FD), F32),
            pltpu.VMEM((TICKS, NH, HT, FD), F32),
            dma((6,)),
            dma((2,)),
            dma((2,)),
            dma((2,)),
            dma((TICKS, NH)),
            dma((TICKS, NH, NP)),
            dma((TICKS, NH)),
            dma((TICKS, NH, NP)),
            dma((TICKS, NH)),
            dma((TICKS, NH)),
            dma((TICKS, NH)),
            dma((TICKS, NH)),
            dma(()),
        ],
        compiler_params=pltpu.CompilerParams(
            collective_id=0, has_side_effects=True, vmem_limit_bytes=56 << 20
        ),
    )(fresh_acts, carried, norm_gain, w_in, taps, filter_taps, decay_rate, w_out4)


def solution(mesh):
    return jax.shard_map(
        body,
        mesh=mesh,
        in_specs=(
            P(None, None, "dp"),
            P("section", None, "dp"),
            P("section", None),
            P("section", None, "dp", None),
            P("section", None, "dp", None),
            P("section", "dp", None),
            P("section", "dp"),
            P("section", None, "dp"),
        ),
        out_specs=P("section", None, None, "dp"),
        check_vma=False,
    )
```

```python
import jax
import jax.numpy as jnp
from jax import lax
from jax.experimental import pallas as pl
from jax.experimental.pallas import tpu as pltpu
from jax.sharding import PartitionSpec as P

EPS = 1e-06
MESH = pl.DeviceIdType.MESH
F32 = jnp.float32
BF16 = jnp.bfloat16

NZ, NX, NS = 8, 4, 8
NP = NZ * NX
TICKS, SEQ, FD, CD, D = 3, 128, 128, 64, 8192
NH, BT = 2, 32
Z_ORDER = (1, 7, 2, 6, 3, 5, 4)
X_ORDER = (2, 1, 3)
SLABS = (0,) + Z_ORDER
NEAR = (1, 7, 2, 6)
DIRECT = ((0, 2), (1, 0), (7, 0), (2, 0), (6, 0), (3, 0), (5, 0), (4, 0))
STEPS = (0, 1, 7, "across", 2, 6, 3, 5, 4)


def kernel(
    fresh, carried, gain, w_in, taps_hbm, long_hbm, decay_hbm, w_out, out,
    acts, gated, produced, final_v, result, w1, w2, gain_v, fresh_v, carried_v,
    taps_v, long_v, decay_v, taps_row, long_row, u_pad, p_pad,
    sem_in, sem_own, sem_xsend, sem_xrecv, a_send, a_recv, y_send, y_recv,
    u_send, u_recv, p_send, p_recv, o_send, o_recv, sem_out,
):
    s = lax.axis_index("section")
    d = lax.axis_index("dp")
    z, x, c = d // 8, (d // 2) % 4, d % 2
    nxt, prv = (s + 1) % NS, (s + NS - 1) % NS

    def dev(sec, dz, dx, core):
        return (sec, ((z + dz) % NZ) * 8 + ((x + dx) % NX) * 2 + core)

    sibling = dev(s, 0, 0, 1 - c)

    def remote(src, dst, send, recv, target):
        return pltpu.make_async_remote_copy(
            src_ref=src, dst_ref=dst, send_sem=send, recv_sem=recv,
            device_id=target, device_id_type=MESH,
        )

    def local(src, dst, sem):
        return pltpu.make_async_copy(src, dst, sem)

    def piece_of(j):
        dz, dx = j // NX, j % NX
        return ((z + NZ - dz) % NZ) * NX + (x + NX - dx) % NX

    mine = pl.ds(pl.multiple_of(c * FD, FD), FD)
    other = pl.ds(pl.multiple_of((1 - c) * FD, FD), FD)

    in_gain = local(gain, gain_v, sem_in.at[0])
    keep = []
    for h in range(NH):
        keep.append(local(carried.at[2 * h + c], carried_v.at[h, :, mine], sem_own.at[0]))
        keep.append(local(fresh.at[0, 2 * h + c], fresh_v.at[0, h, :, mine], sem_own.at[1]))
    for copy in keep:
        copy.start()

    barrier = pltpu.get_barrier_semaphore()
    peers = [sibling]
    for sec in (nxt, prv):
        peers += [dev(sec, dz, 0, c) for dz in range(NZ)]
        peers += [dev(sec, 0, 2, c)]
    peers += [dev(s, dz, 0, c) for dz in range(1, NZ)]
    peers += [dev(s, 0, dx, c) for dx in range(1, NX)]
    for peer in peers:
        pl.semaphore_signal(barrier, inc=1, device_id=peer, device_id_type=MESH)
    in_gain.start()
    pl.semaphore_wait(barrier, len(peers))

    for h in range(NH):
        remote(
            carried.at[2 * h + 1 - c], carried_v.at[h, :, mine], sem_xsend.at[0], sem_xrecv.at[0], sibling
        ).start()
        remote(
            fresh.at[0, 2 * h + 1 - c], fresh_v.at[0, h, :, mine], sem_xsend.at[1], sem_xrecv.at[1], sibling
        ).start()
    pairs = (
        (taps_hbm, taps_v.at[c], 2),
        (long_hbm.at[0], long_v.at[c], 3),
        (decay_hbm, decay_v.at[c], 4),
        (w_in.at[0], w1.at[:, c], 5),
        (w_out, w2.at[:, :, mine], 6),
    )

    def half_wait(sem, ref):
        local(ref, ref, sem).wait()

    half_wait(sem_own.at[0], carried_v.at[:, :, mine])
    half_wait(sem_own.at[1], fresh_v.at[0, :, :, mine])
    half_wait(sem_xrecv.at[0], carried_v.at[:, :, other])
    half_wait(sem_xrecv.at[1], fresh_v.at[0, :, :, other])
    for h in range(NH):
        acts[0, h, 0] = jnp.where(s == 0, fresh_v[0, h], carried_v[h])

    def phase_one(buf, src, send, recv, sec, own):
        for dz, dx in (((0, 0),) if own else ()) + DIRECT:
            j = dz * NX + dx
            remote(src, buf.at[j], send, recv.at[j], dev(sec, dz, dx, c)).start()

    def arrived(buf, recv, j):
        remote(buf.at[j], buf.at[j], recv.at[j], recv.at[j], sibling).wait_recv()

    def phase_two(buf, send, recv, own, slabs):
        for step in slabs:
            if step == "across":
                arrived(buf, recv, 2)
                for dz in NEAR:
                    j = dz * NX + 2
                    remote(buf.at[2], buf.at[j], send, recv.at[j], dev(s, dz, 0, c)).start()
                continue
            j = step * NX
            if step or own:
                arrived(buf, recv, j)
            for dx in X_ORDER:
                if dx == 2 and (step == 0 or step in NEAR):
                    continue
                remote(buf.at[j], buf.at[j + dx], send, recv.at[j + dx], dev(s, 0, dx, c)).start()

    def drain(buf, send, count):
        local(buf.at[pl.ds(0, count)], buf.at[pl.ds(0, count)], send).wait()

    for h in range(NH):
        phase_one(acts.at[0, h], acts.at[0, h, 0], a_send.at[0, h], a_recv.at[0, h], s, False)

    for src, dst, n in pairs:
        local(src, dst, sem_own.at[n]).start()
        remote(src, dst, sem_xsend.at[n], sem_xrecv.at[n], sibling).start()
    for k in range(1, TICKS):
        for h in range(NH):
            local(fresh.at[k, 2 * h + c], fresh_v.at[k, h, :, mine], sem_own.at[7]).start()
            remote(
                fresh.at[k, 2 * h + 1 - c], fresh_v.at[k, h, :, mine], sem_xsend.at[7], sem_xrecv.at[7], sibling
            ).start()

    for h in range(NH):
        phase_two(acts.at[0, h], a_send.at[0, h], a_recv.at[0, h], False, STEPS)

    in_gain.wait()
    for src, dst, n in pairs:
        local(src, dst, sem_own.at[n]).wait()
        remote(src, dst, sem_xsend.at[n], sem_xrecv.at[n], sibling).wait_recv()
    later = pl.ds(1, TICKS - 1)
    half_wait(sem_own.at[7], fresh_v.at[later, :, :, mine])
    half_wait(sem_xrecv.at[7], fresh_v.at[later, :, :, other])

    for i in range(3):
        for j in range(3):
            taps_row[pl.ds(j, 1), pl.ds(i * 128, 128)] = jnp.concatenate(
                [taps_v[0, i, j], taps_v[1, i, j]], axis=1
            )
    tall = jnp.concatenate([long_v[0], long_v[1]], axis=0).T
    decay_all = jnp.concatenate([decay_v[0], decay_v[1]], axis=1)
    lag = lax.broadcasted_iota(jnp.int32, (128, 128), 0).astype(F32)
    long_row[...] = tall * jnp.exp(-decay_all * lag)
    for k in range(TICKS):
        p_pad[k, pl.ds(0, BT), :] = jnp.zeros((BT, 128), F32)

    @pl.when(c == 0)
    def _():
        for k in range(TICKS):
            u_pad[k, 0, pl.ds(0, 8), :] = jnp.zeros((8, 384), F32)

    def tail_copy(k, h, cc):
        to = h + cc
        return remote(
            u_pad.at[k, h, pl.ds(BT, 8)], u_pad.at[k, to, pl.ds(0, 8)],
            u_send.at[k, h], u_recv.at[k, to], sibling,
        )

    def history_copy(k, b):
        rows = pl.ds(BT + b * BT, BT)
        return remote(
            p_pad.at[k, rows], p_pad.at[k, rows], p_send.at[k, b], p_recv.at[k, b], sibling
        )

    def spread(k, h, slabs):
        phase_two(acts.at[k, h], a_send.at[k, h], a_recv.at[k, h], k > 0, slabs)

    def project(k, h):
        buf, recv = acts.at[k, h], a_recv.at[k, h]
        squares = jnp.zeros((BT, 256), F32)
        total = jnp.zeros((BT, 384), F32)
        for dz in SLABS:
            for dx in (0,) + X_ORDER:
                j = dz * NX + dx
                if dx and j != 2:
                    arrived(buf, recv, j)
                wide = buf[j].astype(F32)
                cols = pl.ds(pl.multiple_of(piece_of(j) * 256, 256), 256)
                normed = (wide * gain_v[:, cols]).astype(BF16)
                squares = squares + wide * wide
                w = w1[:, :, :, cols].reshape(384, 256)
                total = total + lax.dot_general(
                    normed, w, (((1,), (1,)), ((), ())), preferred_element_type=F32
                )
        factor = lax.rsqrt(jnp.sum(squares, axis=1, keepdims=True) / D + EPS)
        u_pad[k, h, pl.ds(8, BT), :] = total * factor
        for cc in range(2):
            if h + cc < NH:
                @pl.when(c == cc)
                def _():
                    tail_copy(k, h, cc).start()

    def mix(k, h):
        for cc in range(2):
            b = 2 * h + cc

            @pl.when(c == cc)
            def _():
                if b:
                    tail = u_pad.at[k, h, pl.ds(0, 8)]
                    remote(tail, tail, u_recv.at[k, h], u_recv.at[k, h], sibling).wait_recv()
                mixed = taps_row[0:1, :] * u_pad[k, h, pl.ds(8, BT), :]
                for j in range(1, 3):
                    mixed = mixed + taps_row[j:j + 1, :] * u_pad[k, h, pl.ds(8 - j, BT), :]
                p_pad[k, pl.ds(BT + b * BT, BT), :] = mixed[:, 128:256] * mixed[:, 256:384]
                if b < 3:
                    history_copy(k, b).start()
                if b:
                    history_copy(k, b - 1).wait_recv()
                conv = jnp.zeros((BT, 128), F32)
                for j in range(BT * (b + 1)):
                    conv = conv + long_row[j:j + 1, :] * p_pad[k, pl.ds(BT + b * BT - j, BT), :]
                gated[k, h, 0] = (mixed[:, 0:128] * conv).astype(BF16)

        phase_one(gated.at[k, h], gated.at[k, h, 0], y_send.at[k, h], y_recv.at[k, h], s, False)

    def spread_gated(k, h, slabs):
        phase_two(gated.at[k, h], y_send.at[k, h], y_recv.at[k, h], False, slabs)

    def combine(k, h):
        buf, recv = gated.at[k, h], y_recv.at[k, h]
        total = jnp.zeros((BT, 256), F32)
        for dz in SLABS:
            for dx in X_ORDER:
                if dz or dx != 2:
                    arrived(buf, recv, dz * NX + dx)
            js = [dz * NX + dx for dx in range(NX)]
            lhs = jnp.concatenate([buf[j] for j in js], axis=1)
            rhs = jnp.concatenate([w2[piece_of(j)] for j in js], axis=0)
            total = total + jnp.dot(lhs, rhs, preferred_element_type=F32)
        final = (total + acts[k, h, 0].astype(F32)).astype(BF16)
        if k + 1 < TICKS:
            produced[k, h] = jnp.where(s == NS - 1, fresh_v[k + 1, h], final)
            phase_one(
                acts.at[k + 1, h], produced.at[k, h], a_send.at[k + 1, h], a_recv.at[k + 1, h], nxt, True
            )
        final_v[k, h] = final
        block = 2 * h + c
        result[k, block] = jnp.where(c == 0, final[:, 0:128], final[:, 128:256])
        out_copy(k, h).start()

    def out_copy(k, h):
        block = 2 * h + c
        return remote(
            final_v.at[k, h, :, other], result.at[k, block], o_send.at[k, h], o_recv.at[k, h], sibling
        )

    for k in range(TICKS):
        if k:
            spread(k, 0, STEPS)
            spread(k, 1, STEPS)
        project(k, 0)
        mix(k, 0)
        project(k, 1)
        mix(k, 1)
        spread_gated(k, 0, STEPS)
        spread_gated(k, 1, STEPS)
        combine(k, 0)
        combine(k, 1)

    for k in range(TICKS):
        for h in range(NH):
            out_copy(k, h).wait_recv()
    put = local(result, out, sem_out)
    put.start()
    for src, dst, n in pairs:
        remote(src, dst, sem_xsend.at[n], sem_xrecv.at[n], sibling).wait_send()
    half_wait(sem_xsend.at[0], carried_v.at[:, :, other])
    half_wait(sem_xsend.at[1], fresh_v.at[0, :, :, other])
    half_wait(sem_xsend.at[7], fresh_v.at[later, :, :, other])
    for k in range(TICKS):
        for h in range(NH):
            out_copy(k, h).wait_send()
            drain(acts.at[k, h], a_send.at[k, h], NP if k else NP - 1)
            drain(gated.at[k, h], y_send.at[k, h], NP - 1)
            for cc in range(2):
                if 2 * h + cc < 3:
                    @pl.when(c == cc)
                    def _():
                        tail_copy(k, h, cc).wait_send()
                        history_copy(k, 2 * h + cc).wait_send()
    put.wait()


def body(fresh_acts, carried, norm_gain, w_in, short_filter, filter_taps, decay_rate, w_out):
    blocks = SEQ // BT
    fresh = fresh_acts.reshape(TICKS, blocks, BT, FD)
    waiting = carried.reshape(blocks, BT, FD)
    w_out3 = w_out.reshape(NP, 2 * CD, FD)
    taps = jnp.transpose(short_filter, (1, 3, 0, 2))
    any_spec = pl.BlockSpec(memory_space=pl.ANY)
    dma = pltpu.SemaphoreType.DMA
    made = pl.pallas_call(
        kernel,
        name="relay",
        out_shape=jax.ShapeDtypeStruct((TICKS, blocks, BT, FD), BF16),
        in_specs=[any_spec] * 8,
        out_specs=any_spec,
        scratch_shapes=[
            pltpu.VMEM((TICKS, NH, NP, BT, 256), BF16),
            pltpu.VMEM((TICKS, NH, NP, BT, 128), BF16),
            pltpu.VMEM((TICKS - 1, NH, BT, 256), BF16),
            pltpu.VMEM((TICKS, NH, BT, 256), BF16),
            pltpu.VMEM((TICKS, blocks, BT, FD), BF16),
            pltpu.VMEM((3, 2, CD, D), BF16),
            pltpu.VMEM((NP, 128, 256), BF16),
            pltpu.VMEM((1, D), F32),
            pltpu.VMEM((TICKS, NH, BT, 256), BF16),
            pltpu.VMEM((NH, BT, 256), BF16),
            pltpu.VMEM((2, 3, 3, 1, CD), F32),
            pltpu.VMEM((2, CD, 128), F32),
            pltpu.VMEM((2, 1, CD), F32),
            pltpu.VMEM((8, 384), F32),
            pltpu.VMEM((128, 128), F32),
            pltpu.VMEM((TICKS, NH, 8 + BT, 384), F32),
            pltpu.VMEM((TICKS, BT + SEQ, 128), F32),
            dma((1,)),
            dma((8,)),
            dma((8,)),
            dma((8,)),
            dma((TICKS, NH)),
            dma((TICKS, NH, NP)),
            dma((TICKS, NH)),
            dma((TICKS, NH, NP)),
            dma((TICKS, NH)),
            dma((TICKS, NH)),
            dma((TICKS, 4)),
            dma((TICKS, 4)),
            dma((TICKS, NH)),
            dma((TICKS, NH)),
            dma(()),
        ],
        compiler_params=pltpu.CompilerParams(
            collective_id=0, has_side_effects=True, vmem_limit_bytes=56 << 20
        ),
    )(fresh, waiting, norm_gain, w_in, taps, filter_taps, decay_rate, w_out3)
    return made.reshape(1, TICKS, SEQ, FD)


def solution(mesh):
    return jax.shard_map(
        body,
        mesh=mesh,
        in_specs=(
            P(None, None, "dp"),
            P("section", None, "dp"),
            P("section", None),
            P("section", None, "dp", None),
            P("section", None, "dp", None),
            P("section", "dp", None),
            P("section", "dp"),
            P("section", None, "dp"),
        ),
        out_specs=P("section", None, None, "dp"),
        check_vma=False,
    )
```

```python
import jax
import jax.numpy as jnp
from jax import lax
from jax.experimental import pallas as pl
from jax.experimental.pallas import tpu as pltpu
from jax.sharding import PartitionSpec as P

EPS = 1e-06
MESH = pl.DeviceIdType.MESH
F32 = jnp.float32
BF16 = jnp.bfloat16

NZ, NX, NS = 8, 4, 8
NP = NZ * NX
TICKS, SEQ, FD, CD, D = 3, 128, 128, 64, 8192
NH, BT = 2, 32
Z_ORDER = (1, 7, 2, 6, 3, 5, 4)
X_ORDER = (2, 1, 3)
SLABS = (0,) + Z_ORDER
NEAR = (1, 7, 2, 6)
DIRECT = ((0, 2), (1, 0), (7, 0), (2, 0), (6, 0), (3, 0), (5, 0), (4, 0))
STEPS = (0, 1, 7, "across", 2, 6, 3, 5, 4)


def kernel(
    fresh, carried, gain, w_in, taps_hbm, long_hbm, decay_hbm, w_out, out,
    acts, gated, produced, final_v, result, w1, w2, gain_v, fresh_v, carried_v,
    taps_v, long_v, decay_v, taps_row, long_row, u_pad, p_pad,
    sem_in, sem_own, sem_xsend, sem_xrecv, a_send, a_recv, y_send, y_recv,
    u_send, u_recv, p_send, p_recv, o_send, o_recv, sem_out,
):
    s = lax.axis_index("section")
    d = lax.axis_index("dp")
    z, x, c = d // 8, (d // 2) % 4, d % 2
    nxt, prv = (s + 1) % NS, (s + NS - 1) % NS

    def dev(sec, dz, dx, core):
        return (sec, ((z + dz) % NZ) * 8 + ((x + dx) % NX) * 2 + core)

    sibling = dev(s, 0, 0, 1 - c)

    def remote(src, dst, send, recv, target):
        return pltpu.make_async_remote_copy(
            src_ref=src, dst_ref=dst, send_sem=send, recv_sem=recv,
            device_id=target, device_id_type=MESH,
        )

    def local(src, dst, sem):
        return pltpu.make_async_copy(src, dst, sem)

    def piece_of(j):
        dz, dx = j // NX, j % NX
        return ((z + NZ - dz) % NZ) * NX + (x + NX - dx) % NX

    mine = pl.ds(pl.multiple_of(c * FD, FD), FD)
    other = pl.ds(pl.multiple_of((1 - c) * FD, FD), FD)

    in_gain = local(gain, gain_v, sem_in.at[0])
    keep = []
    for h in range(NH):
        keep.append(local(carried.at[2 * h + c], carried_v.at[h, :, mine], sem_own.at[0]))
        keep.append(local(fresh.at[0, 2 * h + c], fresh_v.at[0, h, :, mine], sem_own.at[1]))
    for copy in keep:
        copy.start()

    barrier = pltpu.get_barrier_semaphore()
    peers = [sibling]
    for sec in (nxt, prv):
        peers += [dev(sec, dz, 0, c) for dz in range(NZ)]
        peers += [dev(sec, 0, 2, c)]
    peers += [dev(s, dz, 0, c) for dz in range(1, NZ)]
    peers += [dev(s, 0, dx, c) for dx in range(1, NX)]
    for peer in peers:
        pl.semaphore_signal(barrier, inc=1, device_id=peer, device_id_type=MESH)
    in_gain.start()
    pl.semaphore_wait(barrier, len(peers))

    for h in range(NH):
        remote(
            carried.at[2 * h + 1 - c], carried_v.at[h, :, mine], sem_xsend.at[0], sem_xrecv.at[0], sibling
        ).start()
        remote(
            fresh.at[0, 2 * h + 1 - c], fresh_v.at[0, h, :, mine], sem_xsend.at[1], sem_xrecv.at[1], sibling
        ).start()
    pairs = (
        (taps_hbm, taps_v.at[c], 2),
        (long_hbm.at[0], long_v.at[c], 3),
        (decay_hbm, decay_v.at[c], 4),
        (w_in.at[0], w1.at[:, c], 5),
        (w_out, w2.at[:, :, mine], 6),
    )

    def half_wait(sem, ref):
        local(ref, ref, sem).wait()

    half_wait(sem_own.at[0], carried_v.at[:, :, mine])
    half_wait(sem_own.at[1], fresh_v.at[0, :, :, mine])
    half_wait(sem_xrecv.at[0], carried_v.at[:, :, other])
    half_wait(sem_xrecv.at[1], fresh_v.at[0, :, :, other])
    for h in range(NH):
        acts[0, h, 0] = jnp.where(s == 0, fresh_v[0, h], carried_v[h])

    def phase_one(buf, src, send, recv, sec, own):
        for dz, dx in (((0, 0),) if own else ()) + DIRECT:
            j = dz * NX + dx
            remote(src, buf.at[j], send, recv.at[j], dev(sec, dz, dx, c)).start()

    def arrived(buf, recv, j):
        remote(buf.at[j], buf.at[j], recv.at[j], recv.at[j], sibling).wait_recv()

    def phase_two(buf, send, recv, own, slabs):
        for step in slabs:
            if step == "across":
                arrived(buf, recv, 2)
                for dz in NEAR:
                    j = dz * NX + 2
                    remote(buf.at[2], buf.at[j], send, recv.at[j], dev(s, dz, 0, c)).start()
                continue
            j = step * NX
            if step or own:
                arrived(buf, recv, j)
            for dx in X_ORDER:
                if dx == 2 and (step == 0 or step in NEAR):
                    continue
                remote(buf.at[j], buf.at[j + dx], send, recv.at[j + dx], dev(s, 0, dx, c)).start()

    def drain(buf, send, count):
        local(buf.at[pl.ds(0, count)], buf.at[pl.ds(0, count)], send).wait()

    for h in range(NH):
        phase_one(acts.at[0, h], acts.at[0, h, 0], a_send.at[0, h], a_recv.at[0, h], s, False)

    for src, dst, n in pairs:
        local(src, dst, sem_own.at[n]).start()
        remote(src, dst, sem_xsend.at[n], sem_xrecv.at[n], sibling).start()
    for k in range(1, TICKS):
        for h in range(NH):
            local(fresh.at[k, 2 * h + c], fresh_v.at[k, h, :, mine], sem_own.at[7]).start()
            remote(
                fresh.at[k, 2 * h + 1 - c], fresh_v.at[k, h, :, mine], sem_xsend.at[7], sem_xrecv.at[7], sibling
            ).start()

    for h in range(NH):
        phase_two(acts.at[0, h], a_send.at[0, h], a_recv.at[0, h], False, STEPS)

    in_gain.wait()
    for src, dst, n in pairs:
        local(src, dst, sem_own.at[n]).wait()
        remote(src, dst, sem_xsend.at[n], sem_xrecv.at[n], sibling).wait_recv()
    later = pl.ds(1, TICKS - 1)
    half_wait(sem_own.at[7], fresh_v.at[later, :, :, mine])
    half_wait(sem_xrecv.at[7], fresh_v.at[later, :, :, other])

    for i in range(3):
        for j in range(3):
            taps_row[pl.ds(j, 1), pl.ds(i * 128, 128)] = jnp.concatenate(
                [taps_v[0, i, j], taps_v[1, i, j]], axis=1
            )
    tall = jnp.concatenate([long_v[0], long_v[1]], axis=0).T
    decay_all = jnp.concatenate([decay_v[0], decay_v[1]], axis=1)
    lag = lax.broadcasted_iota(jnp.int32, (128, 128), 0).astype(F32)
    long_row[...] = tall * jnp.exp(-decay_all * lag)
    for k in range(TICKS):
        p_pad[k, pl.ds(0, BT), :] = jnp.zeros((BT, 128), F32)

    @pl.when(c == 0)
    def _():
        for k in range(TICKS):
            u_pad[k, 0, pl.ds(0, 8), :] = jnp.zeros((8, 384), F32)

    def tail_copy(k, h, cc):
        to = h + cc
        return remote(
            u_pad.at[k, h, pl.ds(BT, 8)], u_pad.at[k, to, pl.ds(0, 8)],
            u_send.at[k, h], u_recv.at[k, to], sibling,
        )

    def history_copy(k, b):
        rows = pl.ds(BT + b * BT, BT)
        return remote(
            p_pad.at[k, rows], p_pad.at[k, rows], p_send.at[k, b], p_recv.at[k, b], sibling
        )

    def spread(k, h, slabs):
        phase_two(acts.at[k, h], a_send.at[k, h], a_recv.at[k, h], k > 0, slabs)

    def project(k, h):
        buf, recv = acts.at[k, h], a_recv.at[k, h]
        squares = jnp.zeros((BT, 256), F32)
        total = jnp.zeros((BT, 384), F32)
        for dz in SLABS:
            for dx in (0,) + X_ORDER:
                j = dz * NX + dx
                if dx and j != 2:
                    arrived(buf, recv, j)
                wide = buf[j].astype(F32)
                cols = pl.ds(pl.multiple_of(piece_of(j) * 256, 256), 256)
                normed = (wide * gain_v[:, cols]).astype(BF16)
                squares = squares + wide * wide
                w = w1[:, :, :, cols].reshape(384, 256)
                total = total + lax.dot_general(
                    normed, w, (((1,), (1,)), ((), ())), preferred_element_type=F32
                )
        factor = lax.rsqrt(jnp.sum(squares, axis=1, keepdims=True) / D + EPS)
        u_pad[k, h, pl.ds(8, BT), :] = total * factor
        for cc in range(2):
            if h + cc < NH:
                @pl.when(c == cc)
                def _():
                    tail_copy(k, h, cc).start()

    def mix(k, h):
        for cc in range(2):
            b = 2 * h + cc

            @pl.when(c == cc)
            def _():
                if b:
                    tail = u_pad.at[k, h, pl.ds(0, 8)]
                    remote(tail, tail, u_recv.at[k, h], u_recv.at[k, h], sibling).wait_recv()
                mixed = taps_row[0:1, :] * u_pad[k, h, pl.ds(8, BT), :]
                for j in range(1, 3):
                    mixed = mixed + taps_row[j:j + 1, :] * u_pad[k, h, pl.ds(8 - j, BT), :]
                p_pad[k, pl.ds(BT + b * BT, BT), :] = mixed[:, 128:256] * mixed[:, 256:384]
                if b < 3:
                    history_copy(k, b).start()
                if b:
                    history_copy(k, b - 1).wait_recv()
                conv = jnp.zeros((BT, 128), F32)
                for j in range(BT * (b + 1)):
                    conv = conv + long_row[j:j + 1, :] * p_pad[k, pl.ds(BT + b * BT - j, BT), :]
                gated[k, h, 0] = (mixed[:, 0:128] * conv).astype(BF16)

        phase_one(gated.at[k, h], gated.at[k, h, 0], y_send.at[k, h], y_recv.at[k, h], s, False)

    def spread_gated(k, h, slabs):
        phase_two(gated.at[k, h], y_send.at[k, h], y_recv.at[k, h], False, slabs)

    def combine(k, h):
        buf, recv = gated.at[k, h], y_recv.at[k, h]
        total = jnp.zeros((BT, 256), F32)
        for dz in SLABS:
            for dx in X_ORDER:
                if dz or dx != 2:
                    arrived(buf, recv, dz * NX + dx)
            js = [dz * NX + dx for dx in range(NX)]
            lhs = jnp.concatenate([buf[j] for j in js], axis=1)
            rhs = jnp.concatenate([w2[piece_of(j)] for j in js], axis=0)
            total = total + jnp.dot(lhs, rhs, preferred_element_type=F32)
        final = (total + acts[k, h, 0].astype(F32)).astype(BF16)
        if k + 1 < TICKS:
            produced[k, h] = jnp.where(s == NS - 1, fresh_v[k + 1, h], final)
            phase_one(
                acts.at[k + 1, h], produced.at[k, h], a_send.at[k + 1, h], a_recv.at[k + 1, h], nxt, True
            )
        final_v[k, h] = final
        block = 2 * h + c
        result[k, block] = jnp.where(c == 0, final[:, 0:128], final[:, 128:256])
        out_copy(k, h).start()
        own_copy(k, h).start()

    def own_copy(k, h):
        block = 2 * h + c
        return local(result.at[k, block], out.at[k, block], sem_out.at[k, h])

    def out_copy(k, h):
        block = 2 * h + c
        return remote(
            final_v.at[k, h, :, other], out.at[k, block], o_send.at[k, h], o_recv.at[k, h], sibling
        )

    for k in range(TICKS):
        if k:
            spread(k, 0, STEPS)
            spread(k, 1, STEPS)
        project(k, 0)
        mix(k, 0)
        project(k, 1)
        mix(k, 1)
        spread_gated(k, 0, STEPS)
        spread_gated(k, 1, STEPS)
        combine(k, 0)
        combine(k, 1)

    for src, dst, n in pairs:
        remote(src, dst, sem_xsend.at[n], sem_xrecv.at[n], sibling).wait_send()
    half_wait(sem_xsend.at[0], carried_v.at[:, :, other])
    half_wait(sem_xsend.at[1], fresh_v.at[0, :, :, other])
    half_wait(sem_xsend.at[7], fresh_v.at[later, :, :, other])
    for k in range(TICKS):
        for h in range(NH):
            out_copy(k, h).wait()
            own_copy(k, h).wait()
            drain(acts.at[k, h], a_send.at[k, h], NP if k else NP - 1)
            drain(gated.at[k, h], y_send.at[k, h], NP - 1)
            for cc in range(2):
                if 2 * h + cc < 3:
                    @pl.when(c == cc)
                    def _():
                        tail_copy(k, h, cc).wait_send()
                        history_copy(k, 2 * h + cc).wait_send()


def body(fresh_acts, carried, norm_gain, w_in, short_filter, filter_taps, decay_rate, w_out):
    blocks = SEQ // BT
    fresh = fresh_acts.reshape(TICKS, blocks, BT, FD)
    waiting = carried.reshape(blocks, BT, FD)
    w_out3 = w_out.reshape(NP, 2 * CD, FD)
    taps = jnp.transpose(short_filter, (1, 3, 0, 2))
    any_spec = pl.BlockSpec(memory_space=pl.ANY)
    dma = pltpu.SemaphoreType.DMA
    made = pl.pallas_call(
        kernel,
        name="relay",
        out_shape=jax.ShapeDtypeStruct((TICKS, blocks, BT, FD), BF16),
        in_specs=[any_spec] * 8,
        out_specs=any_spec,
        scratch_shapes=[
            pltpu.VMEM((TICKS, NH, NP, BT, 256), BF16),
            pltpu.VMEM((TICKS, NH, NP, BT, 128), BF16),
            pltpu.VMEM((TICKS - 1, NH, BT, 256), BF16),
            pltpu.VMEM((TICKS, NH, BT, 256), BF16),
            pltpu.VMEM((TICKS, blocks, BT, FD), BF16),
            pltpu.VMEM((3, 2, CD, D), BF16),
            pltpu.VMEM((NP, 128, 256), BF16),
            pltpu.VMEM((1, D), F32),
            pltpu.VMEM((TICKS, NH, BT, 256), BF16),
            pltpu.VMEM((NH, BT, 256), BF16),
            pltpu.VMEM((2, 3, 3, 1, CD), F32),
            pltpu.VMEM((2, CD, 128), F32),
            pltpu.VMEM((2, 1, CD), F32),
            pltpu.VMEM((8, 384), F32),
            pltpu.VMEM((128, 128), F32),
            pltpu.VMEM((TICKS, NH, 8 + BT, 384), F32),
            pltpu.VMEM((TICKS, BT + SEQ, 128), F32),
            dma((1,)),
            dma((8,)),
            dma((8,)),
            dma((8,)),
            dma((TICKS, NH)),
            dma((TICKS, NH, NP)),
            dma((TICKS, NH)),
            dma((TICKS, NH, NP)),
            dma((TICKS, NH)),
            dma((TICKS, NH)),
            dma((TICKS, 4)),
            dma((TICKS, 4)),
            dma((TICKS, NH)),
            dma((TICKS, NH)),
            dma((TICKS, NH)),
        ],
        compiler_params=pltpu.CompilerParams(
            collective_id=0, has_side_effects=True, vmem_limit_bytes=56 << 20
        ),
    )(fresh, waiting, norm_gain, w_in, taps, filter_taps, decay_rate, w_out3)
    return made.reshape(1, TICKS, SEQ, FD)


def solution(mesh):
    return jax.shard_map(
        body,
        mesh=mesh,
        in_specs=(
            P(None, None, "dp"),
            P("section", None, "dp"),
            P("section", None),
            P("section", None, "dp", None),
            P("section", None, "dp", None),
            P("section", "dp", None),
            P("section", "dp"),
            P("section", None, "dp"),
        ),
        out_specs=P("section", None, None, "dp"),
        check_vma=False,
    )
```
